32 devices in a mesh: row: 8 (over z, x), col: 4 (over y, core).
Axes of the slice: x: 2, y: 2, z: 4, core: 2. Of those that a mesh axis runs over, the one named last changes fastest.
Arguments:
- coarse_kernel: bfloat16 [16, 16, 256, 256], P('col', 'row'), may hold values from -0.03125 to 0.03125
- correlations: bfloat16 [128, 256, 256], P('col'), may hold values from -0.375 to 0.375
- coarse_of: int32 [128], replicated, may hold values from 0 to 15
- energy: float32 [32768], P('row'), may hold values from 1 to 8
- start_vectors: float32 [32768, 64], P(('row', 'col')), may hold values from -6 to 6
Outputs:
- hamiltonian: bfloat16 [32768, 32768], P('row', 'col')
- vectors: float32 [32768, 64], P(('row', 'col'))
- gram: float32 [64, 64], replicated
The draws below stay inside these ranges and needn't reach their ends.
All inputs are finite; a program needn't handle non-finite values.
Results may differ from the reference program's by a relative error of at most 0.009.
Values may be sent and summed in bfloat16 or wider, within the bound.
No kernel may reach another device: no remote copies, remote signals or barrier semaphores. Data moves between devices by JAX's collectives and lax.ppermute only.
A program may use at most 320 MiB of HBM per device.

```python
import math
import jax
import jax.numpy as jnp
from jax import lax

NK = 128
NKC = 16
VECS = 64
STEPS = 2
P_SIZE = 256
HAM = 32768


def with_ends(values, stream_key, least, top_value):
    index_at = [jax.random.randint(jax.random.fold_in(stream_key, axis), (), 0, length) for axis, length in enumerate(values.shape)]
    longest = values.shape.index(max(values.shape))
    neighbour = index_at[:longest] + [(index_at[longest] + 1) % values.shape[longest]] + index_at[longest + 1:]
    return values.at[tuple(index_at)].set(least).at[tuple(neighbour)].set(top_value)


def level_of(stream_key, dims, split, least, largest):
    level, own = 1.0, jax.random.fold_in(stream_key, 6)
    for position, parts in split:
        heights = jnp.exp(jax.random.uniform(jax.random.fold_in(own, position), (parts,), jnp.float32, least / len(split), largest / len(split)))
        level = level * jnp.repeat(heights, dims[position] // parts).reshape([-1 if axis == position else 1 for axis in range(len(dims))])
    return level


def noise(own_key, dims, deviation, bound, split=(), held_as=jnp.bfloat16):
    factor_of = level_of(own_key, dims, split, -0.22, 0.18) if split else 1.0
    array = jax.random.normal(own_key, dims, jnp.float32) * deviation * factor_of
    return jnp.minimum(jnp.maximum(array, -bound), bound).astype(held_as)


def setup_inputs(seed: int = 0) -> dict:
    seeds = jax.random.split(jax.random.key(seed), 6)
    return {
        "coarse_kernel": noise(seeds[0], (NKC, NKC, P_SIZE, P_SIZE), (NK * P_SIZE) ** -0.5, 0.03125, ((0, 4), (1, 8))),
        "correlations": noise(seeds[1], (NK, P_SIZE, P_SIZE), P_SIZE ** -0.5, 0.375, ((0, 4),)),
        "coarse_of": with_ends(jax.random.randint(seeds[2], (NK,), 0, NKC), jax.random.fold_in(seeds[2], 1), 0, NKC - 1).astype(jnp.int32),
        "energy": jnp.clip(jnp.exp(math.log(8.0) - 2.0794415 * jax.random.uniform(seeds[3], (HAM,), jnp.float32) ** level_of(seeds[3], (HAM,), ((0, 8),), -0.2, 0.2)), 1.0, 8.0),
        "start_vectors": noise(seeds[4], (HAM, VECS), 1.0, 6.0, ((0, 32),), jnp.float32),
    }


newton_turns = 8

def inverse_root(gram):
    size = gram.shape[0]
    identity = jnp.eye(size, dtype=jnp.float32)
    scale_norm = jnp.sqrt(jnp.sum(gram * gram))
    ymat = gram / scale_norm
    zmat = identity
    for turn_index in range(newton_turns):
        middle = 1.5 * identity - 0.5 * jnp.dot(zmat, ymat, precision=lax.Precision.HIGHEST)
        ymat = jnp.dot(ymat, middle, precision=lax.Precision.HIGHEST)
        zmat = jnp.dot(middle, zmat, precision=lax.Precision.HIGHEST)
    return zmat / jnp.sqrt(scale_norm)

def reference(coarse_kernel, correlations, coarse_of, energy, start_vectors):
    rotations = correlations.astype(jnp.float32)
    width = correlations.shape[1]

    def one_row(carry, fine_index):
        strip = coarse_kernel[coarse_of[fine_index]].astype(jnp.float32)
        left_side = jnp.einsum('pa,bpq->baq', rotations[fine_index], strip).astype(jnp.bfloat16)
        picked = jnp.take(left_side, coarse_of, axis=0).astype(jnp.float32)
        tile_row = jnp.einsum('kpq,kqs->pks', picked, rotations).astype(jnp.bfloat16)
        return (carry, tile_row)
    total = NK * width
    carry_out, tiles = lax.scan(one_row, jnp.zeros((), jnp.float32), jnp.arange(NK, dtype=jnp.int32))
    matrix = tiles.reshape(total, total)
    current = start_vectors
    scale_col = energy[:, None]
    gram = jnp.zeros((current.shape[1], current.shape[1]), jnp.float32)
    for turn_index in range(STEPS):
        image = lax.dot_general(matrix, current.astype(jnp.bfloat16), (((0,), (0,)), ((), ())), preferred_element_type=jnp.float32)
        scaled = (image + scale_col * current) / scale_col
        gram = jnp.dot(scaled.T, scaled, precision=lax.Precision.HIGHEST)
        current = jnp.dot(scaled, inverse_root(gram), precision=lax.Precision.HIGHEST)
    return (matrix, current, gram)
```

```python
import functools

import jax
import jax.numpy as jnp
from jax import lax
from jax.experimental import pallas as pl
from jax.experimental.pallas import tpu as pltpu
from jax.sharding import PartitionSpec as P

STEPS = 2
newton_turns = 8
BF16 = jnp.bfloat16
F32 = jnp.float32
HIGHEST = lax.Precision.HIGHEST


def inverse_root(gram):
    size = gram.shape[0]
    identity = jnp.eye(size, dtype=F32)
    scale_norm = jnp.sqrt(jnp.sum(gram * gram))
    ymat = gram / scale_norm
    zmat = identity
    for turn_index in range(newton_turns):
        middle = 1.5 * identity - 0.5 * jnp.dot(zmat, ymat, precision=HIGHEST)
        ymat = jnp.dot(ymat, middle, precision=HIGHEST)
        zmat = jnp.dot(middle, zmat, precision=HIGHEST)
    return zmat / jnp.sqrt(scale_norm)


def bits_of(size):
    assert size & (size - 1) == 0
    return [1 << i for i in range(size.bit_length() - 1)]


def swap(value, axis, bit):
    return lax.ppermute(value, axis, [(i, i ^ bit) for i in range(lax.axis_size(axis))])


def sum_over(value, axis, dtype):
    for bit in bits_of(lax.axis_size(axis)):
        sent = value.astype(dtype)
        value = sent.astype(F32) + swap(sent, axis, bit).astype(F32)
    return value


def gather_over(value, axis):
    for bit in reversed(bits_of(lax.axis_size(axis))):
        value = jnp.concatenate([value, swap(value, axis, bit)], axis=0)
    return value


def slot_of(source, mine, size):
    count = size.bit_length() - 1
    apart = source ^ mine
    return sum(((apart >> i) & 1) << (count - 1 - i) for i in range(count))


def row_rotations(correlations, fine_rows):
    rows_total, cols_total = lax.axis_size("row"), lax.axis_size("col")
    fine_cols = correlations.shape[0]
    row_index, col_index = lax.axis_index("row"), lax.axis_index("col")
    offset = row_index * fine_rows % fine_cols
    source = row_index * fine_rows // fine_cols
    value = lax.dynamic_slice_in_dim(correlations, offset, fine_rows, 0)
    done = 0
    for bit in reversed(bits_of(cols_total)):
        pairs = []
        for row in range(rows_total):
            home = row * fine_rows // fine_cols
            for col in range(cols_total):
                if (col ^ home) & ~done == 0:
                    pairs.append((row * cols_total + col, row * cols_total + (col ^ bit)))
        got = lax.ppermute(value, ("row", "col"), pairs)
        value = jnp.where((col_index ^ source) & bit != 0, got, value)
        done |= bit
    return value


def tiles_kernel(n_col, first_col, coarse_ref, place_ref, rot_ref, corr_ref, kern_ref, *rest):
    out_ref, kbuf, rott, left, tile, count, ksem, osem = rest[-8:]
    sources = kern_ref.shape[0]
    fine_rows, width = rot_ref.shape[0], rot_ref.shape[1]
    fine_cols = corr_ref.shape[0]
    per_src = kern_ref.shape[1]
    cols_total = kbuf.shape[1]
    groups = sources // cols_total
    rows = fine_rows * width
    row_first = place_ref[0] * fine_rows
    col_first = place_ref[1] * fine_cols

    def fetch(group, slot):
        return pltpu.make_async_copy(
            kern_ref.at[pl.ds(group * cols_total, cols_total)], kbuf.at[slot], ksem.at[slot]
        )

    def flush(slot, column):
        start = pl.multiple_of(column * width, width)
        return pltpu.make_async_copy(
            tile.at[slot], out_ref.at[:, pl.ds(start, width)], osem.at[slot]
        )

    fetch(0, 0).start()
    count[0] = 0
    for k in range(fine_rows):
        rott[k] = rot_ref[k].T

    def per_group(group, carry):
        slot = lax.rem(group, 2)
        fetch(group, slot).wait()

        @pl.when(group + 1 < groups)
        def _():
            fetch(group + 1, 1 - slot).start()

        column = group * n_col + first_col
        hits = lax.fori_loop(
            0, fine_cols, lambda m, acc: acc + (coarse_ref[col_first + m] == column).astype(jnp.int32), 0
        )

        @pl.when(hits > 0)
        def _():
            for k in range(fine_rows):
                b = coarse_ref[row_first + k]
                block = kbuf[slot, b // per_src, lax.rem(b, per_src)]
                left[pl.ds(k * width, width), :] = jnp.dot(
                    rott[k], block, preferred_element_type=F32
                ).astype(BF16)

            def per_column(m, inner):
                @pl.when(coarse_ref[col_first + m] == column)
                def _():
                    done = count[0]
                    out_slot = lax.rem(done, 2)

                    @pl.when(done >= 2)
                    def _():
                        flush(out_slot, m).wait()

                    rotation = corr_ref[m]
                    step = 2 * width
                    for part in range(rows // step):
                        here = pl.ds(part * step, step)
                        tile[out_slot, here, :] = jnp.dot(
                            left[here, :], rotation, preferred_element_type=F32
                        ).astype(BF16)
                    flush(out_slot, m).start()
                    count[0] = done + 1

                return inner

            lax.fori_loop(0, fine_cols, per_column, 0)

        return carry

    lax.fori_loop(0, groups, per_group, 0)
    total = count[0]
    for back in (1, 2):

        @pl.when(total >= back)
        def _():
            flush(lax.rem(total - back, 2), 0).wait()


def tiles_call(coarse_of, place, rotations, correlations, kernels, n_col, first_col, cols_total, previous):
    fine_rows, width, _ = rotations.shape
    fine_cols = correlations.shape[0]
    shape = jax.ShapeDtypeStruct((fine_rows * width, fine_cols * width), BF16)
    operands = [coarse_of, place, rotations, correlations, kernels]
    smem = pl.BlockSpec(memory_space=pltpu.SMEM)
    vmem = pl.BlockSpec(memory_space=pltpu.VMEM)
    hbm = pl.BlockSpec(memory_space=pl.ANY)
    in_specs = [smem, smem, vmem, vmem, hbm]
    aliases = {}
    if previous is not None:
        operands.append(previous)
        in_specs.append(hbm)
        aliases = {5: 0}
    flops = 2 * fine_rows * (fine_cols + kernels.shape[0] // cols_total) * width**3
    return pl.pallas_call(
        functools.partial(tiles_kernel, n_col, first_col),
        out_shape=shape,
        in_specs=in_specs,
        out_specs=hbm,
        scratch_shapes=[
            pltpu.VMEM((2, cols_total) + kernels.shape[1:], BF16),
            pltpu.VMEM((fine_rows, width, width), BF16),
            pltpu.VMEM((fine_rows * width, width), BF16),
            pltpu.VMEM((2, fine_rows * width, width), BF16),
            pltpu.SMEM((1,), jnp.int32),
            pltpu.SemaphoreType.DMA((2,)),
            pltpu.SemaphoreType.DMA((2,)),
        ],
        input_output_aliases=aliases,
        cost_estimate=pl.CostEstimate(
            flops=flops // n_col, transcendentals=0, bytes_accessed=2 * shape.size // n_col
        ),
        compiler_params=pltpu.CompilerParams(vmem_limit_bytes=40 << 20),
    )(*operands)


NT = (((1,), (1,)), ((), ()))


def vector_slots(place_ref, fine_rows, cols_total, gathered):
    if not gathered:
        return list(range(fine_rows))
    own = fine_rows // cols_total
    return [slot_of(k // own, place_ref[1], cols_total) * own + k % own for k in range(fine_rows)]


def add_by_coarse(coarse_ref, place_ref, vectors, rot_ref, out_ref, total):
    fine_rows, per_row = rot_ref.shape[0], out_ref.shape[0]
    total[...] = jnp.zeros_like(total)
    for k in range(fine_rows):
        where = coarse_ref[place_ref[0] * fine_rows + k] - place_ref[1] * per_row

        @pl.when(jnp.logical_and(where >= 0, where < per_row))
        def _():
            total[where] += lax.dot_general(vectors(k), rot_ref[k], NT, preferred_element_type=F32)

    out_ref[...] = total[...].astype(BF16)


def start_kernel(cols_total, coarse_ref, place_ref, vec_ref, rot_ref, out_ref, total):
    slots = vector_slots(place_ref, rot_ref.shape[0], cols_total, True)
    add_by_coarse(coarse_ref, place_ref, lambda k: vec_ref[slots[k]], rot_ref, out_ref, total)


def step_kernel(rows_total, cols_total, gathered, coarse_ref, place_ref, z_ref, rot_ref, energy_ref, vec_ref, new_ref, gram_ref, *rest):
    fine_rows = rot_ref.shape[0]
    per_col = z_ref.shape[0] // rows_total
    slots = vector_slots(place_ref, fine_rows, cols_total, gathered)
    gram = jnp.zeros(gram_ref.shape, F32)
    for k in range(fine_rows):
        column = coarse_ref[place_ref[0] * fine_rows + k]
        z = z_ref[slot_of(column // per_col, place_ref[0], rows_total) * per_col + lax.rem(column, per_col)]
        image = jnp.dot(z, rot_ref[k], preferred_element_type=F32)
        scale = energy_ref[pl.ds(k, 1), :]
        scaled = (image + scale * vec_ref[slots[k]].astype(F32)) / scale
        new_ref[k] = scaled
        gram = gram + lax.dot_general(scaled, scaled, NT, precision=HIGHEST, preferred_element_type=F32)
    gram_ref[...] = gram
    if rest:
        out_ref, total = rest
        add_by_coarse(coarse_ref, place_ref, lambda k: new_ref[k].astype(BF16), rot_ref, out_ref, total)


def coarse_kernel_product(sums_ref, kern_ref, out_ref):
    per_row, per_col = kern_ref.shape[0], kern_ref.shape[1]
    for j in range(per_col):
        out_ref[j] = sum(
            jnp.dot(sums_ref[i], kern_ref[i, j], preferred_element_type=F32) for i in range(per_row)
        )


def per_device(coarse_kernel, correlations, coarse_of, energy, start_vectors):
    rows_total, cols_total = lax.axis_size("row"), lax.axis_size("col")
    row_index, col_index = lax.axis_index("row"), lax.axis_index("col")
    fine_total = coarse_of.shape[0]
    fine_rows = fine_total // rows_total
    fine_cols = correlations.shape[0]
    width = correlations.shape[1]
    vecs = start_vectors.shape[1]
    per_row, per_col = coarse_kernel.shape[:2]
    smem = pl.BlockSpec(memory_space=pltpu.SMEM)
    vmem = pl.BlockSpec(memory_space=pltpu.VMEM)

    gathered = [
        lax.all_gather(coarse_kernel[:, j], ("row", "col"), axis=0, tiled=False)
        for j in range(per_col)
    ]
    place = jnp.stack([row_index, col_index]).astype(jnp.int32)
    rotations = row_rotations(correlations, fine_rows)

    hamiltonian = None
    for j in range(per_col):
        hamiltonian = tiles_call(
            coarse_of, place, rotations, correlations, gathered[j], per_col, j, cols_total, hamiltonian
        )

    own = fine_rows // cols_total
    vectors = start_vectors.reshape(own, width, vecs).transpose(0, 2, 1).astype(BF16)
    vectors = gather_over(vectors, "col")
    energies = energy.reshape(fine_rows, width)
    sums_shape = jax.ShapeDtypeStruct((per_row, vecs, width), BF16)
    total = pltpu.VMEM((per_row, vecs, width), F32)

    sums = pl.pallas_call(
        functools.partial(start_kernel, cols_total),
        out_shape=sums_shape,
        in_specs=[smem, smem, vmem, vmem],
        out_specs=vmem,
        scratch_shapes=[total],
    )(coarse_of, place, vectors, rotations)
    grams = []
    for turn_index in range(STEPS):
        last = turn_index == STEPS - 1
        sums = sum_over(sums, "row", BF16).astype(BF16)
        partial = pl.pallas_call(
            coarse_kernel_product,
            out_shape=jax.ShapeDtypeStruct((per_col, vecs, width), F32),
            in_specs=[vmem, vmem],
            out_specs=vmem,
        )(sums, coarse_kernel)
        z = gather_over(sum_over(partial, "col", BF16).astype(BF16), "row")
        shapes = [
            jax.ShapeDtypeStruct((fine_rows, vecs, width), F32),
            jax.ShapeDtypeStruct((vecs, vecs), F32),
        ]
        results = pl.pallas_call(
            functools.partial(step_kernel, rows_total, cols_total, turn_index == 0),
            out_shape=shapes if last else shapes + [sums_shape],
            in_specs=[smem, smem, vmem, vmem, vmem, vmem],
            out_specs=[vmem] * (2 if last else 3),
            scratch_shapes=[] if last else [total],
        )(coarse_of, place, z, rotations, energies, vectors)
        vectors = results[0]
        grams.append(sum_over(results[1], "row", F32))
        if not last:
            sums = results[2]
    gram = grams[0]
    root = inverse_root(gram)
    for later in grams[1:]:
        gram = jnp.dot(root.T, jnp.dot(later, root, precision=HIGHEST), precision=HIGHEST)
        root = jnp.dot(root, inverse_root(gram), precision=HIGHEST)
    mine = lax.dynamic_slice_in_dim(vectors, col_index * own, own, 0)
    current = jnp.einsum("kva,vw->kaw", mine, root, precision=HIGHEST, preferred_element_type=F32)
    return hamiltonian, current.reshape(own * width, vecs), gram


def solution(mesh):
    return jax.shard_map(
        per_device,
        mesh=mesh,
        in_specs=(
            P("col", "row", None, None),
            P("col", None, None),
            P(),
            P("row"),
            P(("row", "col"), None),
        ),
        out_specs=(P("row", "col"), P(("row", "col"), None), P()),
        check_vma=False,
    )
```

```python
import functools

import jax
import jax.numpy as jnp
from jax import lax
from jax.experimental import pallas as pl
from jax.experimental.pallas import tpu as pltpu
from jax.sharding import PartitionSpec as P

STEPS = 2
newton_turns = 8
BF16 = jnp.bfloat16
F32 = jnp.float32
HIGHEST = lax.Precision.HIGHEST


def inverse_root(gram):
    size = gram.shape[0]
    identity = jnp.eye(size, dtype=F32)
    scale_norm = jnp.sqrt(jnp.sum(gram * gram))
    ymat = gram / scale_norm
    zmat = identity
    for turn_index in range(newton_turns):
        middle = 1.5 * identity - 0.5 * jnp.dot(zmat, ymat, precision=HIGHEST)
        ymat = jnp.dot(ymat, middle, precision=HIGHEST)
        zmat = jnp.dot(middle, zmat, precision=HIGHEST)
    return zmat / jnp.sqrt(scale_norm)


def next_root(gram, before):
    if before is None:
        return gram, inverse_root(gram)
    gram = jnp.dot(before.T, jnp.dot(gram, before, precision=HIGHEST), precision=HIGHEST)
    return gram, jnp.dot(before, inverse_root(gram), precision=HIGHEST)


def bits_of(size):
    assert size & (size - 1) == 0
    return [1 << i for i in range(size.bit_length() - 1)]


def swap(value, axis, bit):
    return lax.ppermute(value, axis, [(i, i ^ bit) for i in range(lax.axis_size(axis))])


def sum_over(value, axis, dtype):
    for bit in bits_of(lax.axis_size(axis)):
        sent = value.astype(dtype)
        value = sent.astype(F32) + swap(sent, axis, bit).astype(F32)
    return value


def spread(value, axis):
    size = lax.axis_size(axis)
    return [value] + [swap(value, axis, bits) for bits in range(1, size)]


def tree_sum(values):
    while len(values) > 1:
        values = [left + right for left, right in zip(values[::2], values[1::2])]
    return values[0]


def scatter_sum(value, axis):
    for bit in reversed(bits_of(lax.axis_size(axis))):
        half = value.shape[0] // 2
        got = swap(value[half:].astype(BF16), axis, bit)
        value = value[:half].astype(F32) + got.astype(F32)
    return value


def gather_over(value, axis):
    for bit in reversed(bits_of(lax.axis_size(axis))):
        value = jnp.concatenate([value, swap(value, axis, bit)], axis=0)
    return value


def slot_of(source, mine, size):
    count = size.bit_length() - 1
    apart = source ^ mine
    return sum(((apart >> i) & 1) << (count - 1 - i) for i in range(count))


def row_rotations(correlations, fine_rows):
    rows_total, cols_total = lax.axis_size("row"), lax.axis_size("col")
    fine_cols = correlations.shape[0]
    row_index, col_index = lax.axis_index("row"), lax.axis_index("col")
    offset = row_index * fine_rows % fine_cols
    source = row_index * fine_rows // fine_cols
    value = lax.dynamic_slice_in_dim(correlations, offset, fine_rows, 0)
    hops = list(reversed(bits_of(cols_total)))

    def hop(value, bit, done, after):
        pairs = []
        for row in range(rows_total):
            home = row * fine_rows // fine_cols
            for col in range(cols_total):
                if (col ^ home) & ~done == 0:
                    pairs.append((row * cols_total + col, row * cols_total + (col ^ bit)))
        after, value = lax.optimization_barrier((after, value))
        return value, lax.ppermute(value, ("row", "col"), pairs), after

    def take(value, got, bit, after):
        after, got = lax.optimization_barrier((after, got))
        return jnp.where((col_index ^ source) & bit != 0, got, value), after

    return value, hops, hop, take


DEPTH = 3


def tiles_kernel(coarse_ref, place_ref, rot_ref, corr_ref, kern_ref, out_ref, kbuf, rott, corr, left, tile, order, starts, wanted, needed, ksem, rsem, csem, osem):
    sources, per_row, per_col = kern_ref.shape[:3]
    blocks = kbuf.shape[1]
    cols_total = blocks // per_row
    columns = sources // cols_total * per_col
    fine_rows, width = rot_ref.shape[:2]
    fine_cols = corr_ref.shape[0]
    rows = fine_rows * width
    row_first = place_ref[0] * fine_rows
    col_first = place_ref[1] * fine_cols

    rot_copy = pltpu.make_async_copy(rot_ref, rott, rsem.at[0])
    corr_copy = pltpu.make_async_copy(corr_ref, corr, csem.at[0])
    rot_copy.start()
    for b in range(blocks):
        needed[b] = 0
    for column in range(columns):
        starts[column] = 0
    for k in range(fine_rows):
        needed[coarse_ref[row_first + k]] = 1
    for m in range(fine_cols):
        column = coarse_ref[col_first + m]
        starts[column] = starts[column] + 1
    here, found = jnp.int32(0), jnp.int32(0)
    for column in range(columns):
        size = starts[column]
        starts[column] = here
        wanted[found] = column
        here = here + size
        found = found + (size > 0).astype(jnp.int32)
    for m in range(fine_cols):
        column = coarse_ref[col_first + m]
        spot = starts[column]
        order[spot] = m
        starts[column] = spot + 1

    def fetch(turn, act):
        column = wanted[turn]
        slot = lax.rem(turn, DEPTH)
        for b in range(blocks):

            @pl.when(needed[b] > 0)
            def _():
                source = column // per_col * cols_total + b // per_row
                act(
                    pltpu.make_async_copy(
                        kern_ref.at[source, b % per_row, lax.rem(column, per_col)],
                        kbuf.at[slot, b],
                        ksem.at[slot, b],
                    )
                )

    def flush(spot, m):
        slot = lax.rem(spot, DEPTH)
        start = pl.multiple_of(m * width, width)
        return pltpu.make_async_copy(tile.at[slot], out_ref.at[:, pl.ds(start, width)], osem.at[slot])

    for turn in range(DEPTH - 1):

        @pl.when(turn < found)
        def _():
            fetch(turn, lambda copy: copy.start())

    corr_copy.start()
    rot_copy.wait()
    corr_copy.wait()

    def per_tile(spot, turn):
        m = order[spot]
        column = coarse_ref[col_first + m]
        before = coarse_ref[col_first + order[jnp.maximum(spot - 1, 0)]]
        fresh = jnp.logical_or(spot == 0, column != before)

        @pl.when(fresh)
        def _():
            fetch(turn, lambda copy: copy.wait())

            @pl.when(turn + DEPTH - 1 < found)
            def _():
                fetch(turn + DEPTH - 1, lambda copy: copy.start())

            slot = lax.rem(turn, DEPTH)
            for k in range(fine_rows):
                block = kbuf[slot, coarse_ref[row_first + k]]
                left[pl.ds(k * width, width), :] = jnp.dot(
                    rott[k], block, preferred_element_type=F32
                ).astype(BF16)

        @pl.when(spot >= DEPTH)
        def _():
            flush(spot, m).wait()

        out_slot = lax.rem(spot, DEPTH)
        rotation = corr[m]
        step = 4 * width
        for part in range(rows // step):
            some = pl.ds(part * step, step)
            tile[out_slot, some, :] = jnp.dot(
                left[some, :], rotation, preferred_element_type=F32
            ).astype(BF16)
        flush(spot, m).start()
        return turn + fresh.astype(jnp.int32)

    lax.fori_loop(0, fine_cols, per_tile, jnp.int32(0))
    for spot in range(max(fine_cols - DEPTH, 0), fine_cols):
        flush(spot, 0).wait()


def tiles_call(coarse_of, place, rotations, correlations, kernels, cols_total):
    fine_rows, width, _ = rotations.shape
    fine_cols = correlations.shape[0]
    blocks = cols_total * kernels.shape[1]
    columns = kernels.shape[0] // cols_total * kernels.shape[2]
    shape = jax.ShapeDtypeStruct((fine_rows * width, fine_cols * width), BF16)
    smem = pl.BlockSpec(memory_space=pltpu.SMEM)
    hbm = pl.BlockSpec(memory_space=pl.ANY)
    return pl.pallas_call(
        tiles_kernel,
        out_shape=shape,
        in_specs=[smem, smem, hbm, hbm, hbm],
        out_specs=hbm,
        scratch_shapes=[
            pltpu.VMEM((DEPTH, blocks, width, width), BF16),
            pltpu.VMEM(rotations.shape, BF16),
            pltpu.VMEM(correlations.shape, BF16),
            pltpu.VMEM((fine_rows * width, width), BF16),
            pltpu.VMEM((DEPTH, fine_rows * width, width), BF16),
            pltpu.SMEM((fine_cols,), jnp.int32),
            pltpu.SMEM((columns,), jnp.int32),
            pltpu.SMEM((columns + 1,), jnp.int32),
            pltpu.SMEM((blocks,), jnp.int32),
            pltpu.SemaphoreType.DMA((DEPTH, blocks)),
            pltpu.SemaphoreType.DMA((1,)),
            pltpu.SemaphoreType.DMA((1,)),
            pltpu.SemaphoreType.DMA((DEPTH,)),
        ],
        cost_estimate=pl.CostEstimate(
            flops=2 * fine_rows * (fine_cols + columns) * width**3,
            transcendentals=0,
            bytes_accessed=2 * (shape.size + kernels.size),
        ),
        compiler_params=pltpu.CompilerParams(vmem_limit_bytes=40 << 20),
    )(coarse_of, place, rotations, correlations, kernels)


NT = (((1,), (1,)), ((), ()))


def vector_slots(place_ref, fine_rows, cols_total, gathered):
    if not gathered:
        return list(range(fine_rows))
    own = fine_rows // cols_total
    return [slot_of(k // own, place_ref[1], cols_total) * own + k % own for k in range(fine_rows)]


def add_by_coarse(coarse_ref, place_ref, vectors, rot_ref, out_ref, total):
    fine_rows, per_row = rot_ref.shape[0], out_ref.shape[0]
    total[...] = jnp.zeros_like(total)
    for k in range(fine_rows):
        where = coarse_ref[place_ref[0] * fine_rows + k] - place_ref[1] * per_row

        @pl.when(jnp.logical_and(where >= 0, where < per_row))
        def _():
            total[where] += lax.dot_general(vectors(k), rot_ref[k], NT, preferred_element_type=F32)

    out_ref[...] = total[...].astype(BF16)


def start_kernel(rows_total, per_row, coarse_ref, place_ref, vec_ref, rot_ref, out_ref, total):
    own = vec_ref.shape[0]
    total[...] = jnp.zeros_like(total)
    first = (place_ref[1] * rows_total + place_ref[0]) * own
    for k in range(own):
        b = coarse_ref[first + k]
        where = (b // per_row ^ place_ref[1]) * per_row + lax.rem(b, per_row)
        total[where] += lax.dot_general(vec_ref[k], rot_ref[k], NT, preferred_element_type=F32)
    out_ref[...] = total[...].astype(BF16)


def step_kernel(rows_total, cols_total, gathered, coarse_ref, place_ref, z_ref, rot_ref, energy_ref, vec_ref, new_ref, gram_ref, *rest):
    fine_rows = rot_ref.shape[0]
    per_col = z_ref.shape[0] // rows_total
    slots = vector_slots(place_ref, fine_rows, cols_total, gathered)
    gram = jnp.zeros(gram_ref.shape, F32)
    for k in range(fine_rows):
        column = coarse_ref[place_ref[0] * fine_rows + k]
        z = z_ref[slot_of(column // per_col, place_ref[0], rows_total) * per_col + lax.rem(column, per_col)]
        image = jnp.dot(z, rot_ref[k], preferred_element_type=F32)
        scale = energy_ref[pl.ds(k, 1), :]
        scaled = (image + scale * vec_ref[slots[k]].astype(F32)) / scale
        new_ref[k] = scaled
        gram = gram + lax.dot_general(scaled, scaled, NT, precision=HIGHEST, preferred_element_type=F32)
    gram_ref[...] = gram
    if rest:
        out_ref, total = rest
        add_by_coarse(coarse_ref, place_ref, lambda k: new_ref[k].astype(BF16), rot_ref, out_ref, total)


def coarse_kernel_product(sums_ref, kern_ref, out_ref):
    per_row, per_col = kern_ref.shape[0], kern_ref.shape[1]
    for j in range(per_col):
        out_ref[j] = sum(
            jnp.dot(sums_ref[i], kern_ref[i, j], preferred_element_type=F32) for i in range(per_row)
        )


def per_device(coarse_kernel, correlations, coarse_of, energy, start_vectors):
    rows_total, cols_total = lax.axis_size("row"), lax.axis_size("col")
    row_index, col_index = lax.axis_index("row"), lax.axis_index("col")
    fine_total = coarse_of.shape[0]
    fine_rows = fine_total // rows_total
    fine_cols = correlations.shape[0]
    width = correlations.shape[1]
    vecs = start_vectors.shape[1]
    per_row, per_col = coarse_kernel.shape[:2]
    smem = pl.BlockSpec(memory_space=pltpu.SMEM)
    vmem = pl.BlockSpec(memory_space=pltpu.VMEM)

    place = jnp.stack([row_index, col_index]).astype(jnp.int32)

    kernels = lax.all_gather(coarse_kernel, ("row", "col"))
    own = fine_rows // cols_total
    vectors = start_vectors.reshape(own, width, vecs).transpose(0, 2, 1).astype(BF16)
    moves = [(j, j % rows_total * cols_total + j // rows_total) for j in range(rows_total * cols_total)]
    moved = lax.ppermute(vectors, ("row", "col"), moves)
    moved_rot = lax.dynamic_slice_in_dim(correlations, row_index * own, own, 0)
    vectors = gather_over(vectors, "col")
    energies = energy.reshape(fine_rows, width)
    sums_shape = jax.ShapeDtypeStruct((per_row, vecs, width), BF16)
    total = pltpu.VMEM((per_row, vecs, width), F32)

    sums = pl.pallas_call(
        functools.partial(start_kernel, rows_total, per_row),
        out_shape=jax.ShapeDtypeStruct((cols_total * per_row, vecs, width), BF16),
        in_specs=[smem, smem, vmem, vmem],
        out_specs=vmem,
        scratch_shapes=[pltpu.VMEM((cols_total * per_row, vecs, width), F32)],
    )(coarse_of, place, moved, moved_rot)
    sums = scatter_sum(sums, "col")
    rotations, hops, hop, take = row_rotations(correlations, fine_rows)
    rotations, got, sums = hop(rotations, hops[0], 0, sums)

    root, gram, told = None, None, None
    for turn_index in range(STEPS):
        last = turn_index == STEPS - 1
        sums = sum_over(sums, "row", BF16).astype(BF16)
        if told is not None:
            told, sums = lax.optimization_barrier((told, sums))
            gram, root = next_root(tree_sum(told), root)
        partial = pl.pallas_call(
            coarse_kernel_product,
            out_shape=jax.ShapeDtypeStruct((per_col, vecs, width), F32),
            in_specs=[vmem, vmem],
            out_specs=vmem,
        )(sums, coarse_kernel)
        if turn_index == 0:
            done = hops[0]
            rotations, partial = take(rotations, got, hops[0], partial)
            for bit in hops[1:]:
                rotations, got, partial = hop(rotations, bit, done, partial)
                rotations, _ = take(rotations, got, bit, got)
                done |= bit
        z = gather_over(sum_over(partial, "col", BF16).astype(BF16), "row")
        shapes = [
            jax.ShapeDtypeStruct((fine_rows, vecs, width), F32),
            jax.ShapeDtypeStruct((vecs, vecs), F32),
        ]
        results = pl.pallas_call(
            functools.partial(step_kernel, rows_total, cols_total, turn_index == 0),
            out_shape=shapes if last else shapes + [sums_shape],
            in_specs=[smem, smem, vmem, vmem, vmem, vmem],
            out_specs=[vmem] * (2 if last else 3),
            scratch_shapes=[] if last else [total],
        )(coarse_of, place, z, rotations, energies, vectors)
        vectors = results[0]
        told = spread(results[1], "row")
        if not last:
            sums = results[2]
    turned, vectors = lax.optimization_barrier((rotations.transpose(0, 2, 1), vectors))
    hamiltonian = tiles_call(coarse_of, place, turned, correlations, kernels, cols_total)
    told, hamiltonian = lax.optimization_barrier((told, hamiltonian))
    gram, root = next_root(tree_sum(told), root)
    mine = lax.dynamic_slice_in_dim(vectors, col_index * own, own, 0)
    current = jnp.einsum("kva,vw->kaw", mine, root, precision=HIGHEST, preferred_element_type=F32)
    return hamiltonian, current.reshape(own * width, vecs), gram


def solution(mesh):
    return jax.shard_map(
        per_device,
        mesh=mesh,
        in_specs=(
            P("col", "row", None, None),
            P("col", None, None),
            P(),
            P("row"),
            P(("row", "col"), None),
        ),
        out_specs=(P("row", "col"), P(("row", "col"), None), P()),
        check_vma=False,
    )
```

```python
import functools

import jax
import jax.numpy as jnp
from jax import lax
from jax.experimental import pallas as pl
from jax.experimental.pallas import tpu as pltpu
from jax.sharding import PartitionSpec as P

STEPS = 2
newton_turns = 8
BF16 = jnp.bfloat16
F32 = jnp.float32
HIGHEST = lax.Precision.HIGHEST


def inverse_root(gram):
    size = gram.shape[0]
    identity = jnp.eye(size, dtype=F32)
    scale_norm = jnp.sqrt(jnp.sum(gram * gram))
    ymat = gram / scale_norm
    zmat = identity
    for turn_index in range(newton_turns):
        middle = 1.5 * identity - 0.5 * jnp.dot(zmat, ymat, precision=HIGHEST)
        ymat = jnp.dot(ymat, middle, precision=HIGHEST)
        zmat = jnp.dot(middle, zmat, precision=HIGHEST)
    return zmat / jnp.sqrt(scale_norm)


def next_root(gram, before):
    if before is None:
        return gram, inverse_root(gram)
    gram = jnp.dot(before.T, jnp.dot(gram, before, precision=HIGHEST), precision=HIGHEST)
    return gram, jnp.dot(before, inverse_root(gram), precision=HIGHEST)


def bits_of(size):
    assert size & (size - 1) == 0
    return [1 << i for i in range(size.bit_length() - 1)]


def swap(value, axis, bit):
    return lax.ppermute(value, axis, [(i, i ^ bit) for i in range(lax.axis_size(axis))])


def sum_over(value, axis, dtype):
    for bit in bits_of(lax.axis_size(axis)):
        sent = value.astype(dtype)
        value = sent.astype(F32) + swap(sent, axis, bit).astype(F32)
    return value


def spread(value, axis):
    size = lax.axis_size(axis)
    return [value] + [swap(value, axis, bits) for bits in range(1, size)]


def tree_sum(values):
    while len(values) > 1:
        values = [left + right for left, right in zip(values[::2], values[1::2])]
    return values[0]


def scatter_sum(value, axis):
    for bit in reversed(bits_of(lax.axis_size(axis))):
        half = value.shape[0] // 2
        got = swap(value[half:].astype(BF16), axis, bit)
        value = value[:half].astype(F32) + got.astype(F32)
    return value


def gather_over(value, axis):
    for bit in reversed(bits_of(lax.axis_size(axis))):
        value = jnp.concatenate([value, swap(value, axis, bit)], axis=0)
    return value


def gather_halves(value, axis, beside):
    far, last = bits_of(lax.axis_size(axis))[1:], 1
    for bit in reversed(far):
        value = jnp.concatenate([value, swap(value, axis, bit)], axis=0)
    value, *beside = lax.optimization_barrier((value, *beside))
    return (value, swap(value, axis, last)), beside


def slot_of(source, mine, size):
    count = size.bit_length() - 1
    apart = source ^ mine
    return sum(((apart >> i) & 1) << (count - 1 - i) for i in range(count))


def row_rotations(correlations, fine_rows):
    rows_total, cols_total = lax.axis_size("row"), lax.axis_size("col")
    fine_cols = correlations.shape[0]
    row_index, col_index = lax.axis_index("row"), lax.axis_index("col")
    offset = row_index * fine_rows % fine_cols
    source = row_index * fine_rows // fine_cols
    value = lax.dynamic_slice_in_dim(correlations, offset, fine_rows, 0)
    hops = list(reversed(bits_of(cols_total)))

    def hop(value, bit, done, after):
        pairs = []
        for row in range(rows_total):
            home = row * fine_rows // fine_cols
            for col in range(cols_total):
                if (col ^ home) & ~done == 0:
                    pairs.append((row * cols_total + col, row * cols_total + (col ^ bit)))
        after, value = lax.optimization_barrier((after, value))
        return value, lax.ppermute(value, ("row", "col"), pairs), after

    def take(value, got, bit, after):
        after, got = lax.optimization_barrier((after, got))
        return jnp.where((col_index ^ source) & bit != 0, got, value), after

    return value, hops, hop, take


DEPTH = 3


def tiles_kernel(coarse_ref, place_ref, rot_ref, corr_ref, kern_ref, out_ref, kbuf, rott, corr, left, tile, order, starts, wanted, needed, ksem, rsem, csem, osem):
    sources, per_row, per_col = kern_ref.shape[:3]
    blocks = kbuf.shape[1]
    cols_total = blocks // per_row
    columns = sources // cols_total * per_col
    fine_rows, width = rot_ref.shape[:2]
    fine_cols = corr_ref.shape[0]
    rows = fine_rows * width
    row_first = place_ref[0] * fine_rows
    col_first = place_ref[1] * fine_cols

    rot_copy = pltpu.make_async_copy(rot_ref, rott, rsem.at[0])
    corr_copy = pltpu.make_async_copy(corr_ref, corr, csem.at[0])
    rot_copy.start()
    for b in range(blocks):
        needed[b] = 0
    for column in range(columns):
        starts[column] = 0
    for k in range(fine_rows):
        needed[coarse_ref[row_first + k]] = 1
    for m in range(fine_cols):
        column = coarse_ref[col_first + m]
        starts[column] = starts[column] + 1
    here, found = jnp.int32(0), jnp.int32(0)
    for column in range(columns):
        size = starts[column]
        starts[column] = here
        wanted[found] = column
        here = here + size
        found = found + (size > 0).astype(jnp.int32)
    for m in range(fine_cols):
        column = coarse_ref[col_first + m]
        spot = starts[column]
        order[spot] = m
        starts[column] = spot + 1

    def fetch(turn, act):
        column = wanted[turn]
        slot = lax.rem(turn, DEPTH)
        for b in range(blocks):

            @pl.when(needed[b] > 0)
            def _():
                source = column // per_col * cols_total + b // per_row
                act(
                    pltpu.make_async_copy(
                        kern_ref.at[source, b % per_row, lax.rem(column, per_col)],
                        kbuf.at[slot, b],
                        ksem.at[slot, b],
                    )
                )

    def flush(spot, m):
        slot = lax.rem(spot, DEPTH)
        start = pl.multiple_of(m * width, width)
        return pltpu.make_async_copy(tile.at[slot], out_ref.at[:, pl.ds(start, width)], osem.at[slot])

    for turn in range(DEPTH - 1):

        @pl.when(turn < found)
        def _():
            fetch(turn, lambda copy: copy.start())

    corr_copy.start()
    rot_copy.wait()
    corr_copy.wait()

    def per_tile(spot, turn):
        m = order[spot]
        column = coarse_ref[col_first + m]
        before = coarse_ref[col_first + order[jnp.maximum(spot - 1, 0)]]
        fresh = jnp.logical_or(spot == 0, column != before)

        @pl.when(fresh)
        def _():
            fetch(turn, lambda copy: copy.wait())

            @pl.when(turn + DEPTH - 1 < found)
            def _():
                fetch(turn + DEPTH - 1, lambda copy: copy.start())

            slot = lax.rem(turn, DEPTH)
            for k in range(fine_rows):
                block = kbuf[slot, coarse_ref[row_first + k]]
                left[pl.ds(k * width, width), :] = jnp.dot(
                    rott[k], block, preferred_element_type=F32
                ).astype(BF16)

        @pl.when(spot >= DEPTH)
        def _():
            flush(spot, m).wait()

        out_slot = lax.rem(spot, DEPTH)
        rotation = corr[m]
        step = 4 * width
        for part in range(rows // step):
            some = pl.ds(part * step, step)
            tile[out_slot, some, :] = jnp.dot(
                left[some, :], rotation, preferred_element_type=F32
            ).astype(BF16)
        flush(spot, m).start()
        return turn + fresh.astype(jnp.int32)

    lax.fori_loop(0, fine_cols, per_tile, jnp.int32(0))
    for spot in range(max(fine_cols - DEPTH, 0), fine_cols):
        flush(spot, 0).wait()


def tiles_call(coarse_of, place, rotations, correlations, kernels, cols_total):
    fine_rows, width, _ = rotations.shape
    fine_cols = correlations.shape[0]
    blocks = cols_total * kernels.shape[1]
    columns = kernels.shape[0] // cols_total * kernels.shape[2]
    shape = jax.ShapeDtypeStruct((fine_rows * width, fine_cols * width), BF16)
    smem = pl.BlockSpec(memory_space=pltpu.SMEM)
    hbm = pl.BlockSpec(memory_space=pl.ANY)
    return pl.pallas_call(
        tiles_kernel,
        out_shape=shape,
        in_specs=[smem, smem, hbm, hbm, hbm],
        out_specs=hbm,
        scratch_shapes=[
            pltpu.VMEM((DEPTH, blocks, width, width), BF16),
            pltpu.VMEM(rotations.shape, BF16),
            pltpu.VMEM(correlations.shape, BF16),
            pltpu.VMEM((fine_rows * width, width), BF16),
            pltpu.VMEM((DEPTH, fine_rows * width, width), BF16),
            pltpu.SMEM((fine_cols,), jnp.int32),
            pltpu.SMEM((columns,), jnp.int32),
            pltpu.SMEM((columns + 1,), jnp.int32),
            pltpu.SMEM((blocks,), jnp.int32),
            pltpu.SemaphoreType.DMA((DEPTH, blocks)),
            pltpu.SemaphoreType.DMA((1,)),
            pltpu.SemaphoreType.DMA((1,)),
            pltpu.SemaphoreType.DMA((DEPTH,)),
        ],
        cost_estimate=pl.CostEstimate(
            flops=2 * fine_rows * (fine_cols + columns) * width**3,
            transcendentals=0,
            bytes_accessed=2 * (shape.size + kernels.size),
        ),
        compiler_params=pltpu.CompilerParams(vmem_limit_bytes=40 << 20),
    )(coarse_of, place, rotations, correlations, kernels)


NT = (((1,), (1,)), ((), ()))


def vector_slots(place_ref, fine_rows, cols_total, gathered):
    if not gathered:
        return list(range(fine_rows))
    own = fine_rows // cols_total
    return [slot_of(k // own, place_ref[1], cols_total) * own + k % own for k in range(fine_rows)]


def add_by_coarse(coarse_ref, place_ref, vectors, rot_ref, out_ref, total):
    fine_rows, per_row = rot_ref.shape[0], out_ref.shape[0]
    total[...] = jnp.zeros_like(total)
    for k in range(fine_rows):
        where = coarse_ref[place_ref[0] * fine_rows + k] - place_ref[1] * per_row

        @pl.when(jnp.logical_and(where >= 0, where < per_row))
        def _():
            total[where] += lax.dot_general(vectors(k), rot_ref[k], NT, preferred_element_type=F32)

    out_ref[...] = total[...].astype(BF16)


def start_kernel(rows_total, per_row, coarse_ref, place_ref, vec_ref, rot_ref, out_ref, total):
    own = vec_ref.shape[0]
    total[...] = jnp.zeros_like(total)
    first = (place_ref[1] * rows_total + place_ref[0]) * own
    for k in range(own):
        b = coarse_ref[first + k]
        where = (b // per_row ^ place_ref[1]) * per_row + lax.rem(b, per_row)
        total[where] += lax.dot_general(vec_ref[k], rot_ref[k], NT, preferred_element_type=F32)
    out_ref[...] = total[...].astype(BF16)


def step_kernel(rows_total, cols_total, gathered, coarse_ref, place_ref, near_ref, far_ref, rot_ref, energy_ref, vec_ref, new_ref, gram_ref, *rest):
    fine_rows = rot_ref.shape[0]
    half = near_ref.shape[0]
    per_col = 2 * half // rows_total
    slots = vector_slots(place_ref, fine_rows, cols_total, gathered)
    gram = jnp.zeros(gram_ref.shape, F32)
    for k in range(fine_rows):
        column = coarse_ref[place_ref[0] * fine_rows + k]
        slot = slot_of(column // per_col, place_ref[0], rows_total) * per_col + lax.rem(column, per_col)
        near, far = near_ref[jnp.minimum(slot, half - 1)], far_ref[jnp.maximum(slot - half, 0)]
        z = jnp.where(slot < half, near.astype(F32), far.astype(F32)).astype(BF16)
        image = jnp.dot(z, rot_ref[k], preferred_element_type=F32)
        scale = energy_ref[pl.ds(k, 1), :]
        scaled = (image + scale * vec_ref[slots[k]].astype(F32)) / scale
        new_ref[k] = scaled
        gram = gram + lax.dot_general(scaled, scaled, NT, precision=HIGHEST, preferred_element_type=F32)
    gram_ref[...] = gram
    if rest:
        out_ref, total = rest
        add_by_coarse(coarse_ref, place_ref, lambda k: new_ref[k].astype(BF16), rot_ref, out_ref, total)


def coarse_kernel_product(sums_ref, kern_ref, out_ref):
    per_row, per_col = kern_ref.shape[0], kern_ref.shape[1]
    for j in range(per_col):
        out_ref[j] = sum(
            jnp.dot(sums_ref[i], kern_ref[i, j], preferred_element_type=F32) for i in range(per_row)
        )


def per_device(coarse_kernel, correlations, coarse_of, energy, start_vectors):
    rows_total, cols_total = lax.axis_size("row"), lax.axis_size("col")
    row_index, col_index = lax.axis_index("row"), lax.axis_index("col")
    fine_total = coarse_of.shape[0]
    fine_rows = fine_total // rows_total
    fine_cols = correlations.shape[0]
    width = correlations.shape[1]
    vecs = start_vectors.shape[1]
    per_row, per_col = coarse_kernel.shape[:2]
    smem = pl.BlockSpec(memory_space=pltpu.SMEM)
    vmem = pl.BlockSpec(memory_space=pltpu.VMEM)

    place = jnp.stack([row_index, col_index]).astype(jnp.int32)

    kernels = lax.all_gather(coarse_kernel, ("row", "col"))
    own = fine_rows // cols_total
    vectors = start_vectors.reshape(own, width, vecs).transpose(0, 2, 1).astype(BF16)
    moves = [(j, j % rows_total * cols_total + j // rows_total) for j in range(rows_total * cols_total)]
    moved = lax.ppermute(vectors, ("row", "col"), moves)
    moved_rot = lax.dynamic_slice_in_dim(correlations, row_index * own, own, 0)
    vectors = gather_over(vectors, "col")
    energies = energy.reshape(fine_rows, width)
    sums_shape = jax.ShapeDtypeStruct((per_row, vecs, width), BF16)
    total = pltpu.VMEM((per_row, vecs, width), F32)

    sums = pl.pallas_call(
        functools.partial(start_kernel, rows_total, per_row),
        out_shape=jax.ShapeDtypeStruct((cols_total * per_row, vecs, width), BF16),
        in_specs=[smem, smem, vmem, vmem],
        out_specs=vmem,
        scratch_shapes=[pltpu.VMEM((cols_total * per_row, vecs, width), F32)],
    )(coarse_of, place, moved, moved_rot)
    sums = scatter_sum(sums, "col")
    rotations, hops, hop, take = row_rotations(correlations, fine_rows)
    rotations, got, sums = hop(rotations, hops[0], 0, sums)

    root, gram, told = None, None, None
    for turn_index in range(STEPS):
        last = turn_index == STEPS - 1
        sums = sum_over(sums, "row", BF16).astype(BF16)
        if told is not None:
            told, sums = lax.optimization_barrier((told, sums))
            gram, root = next_root(tree_sum(told), root)
        partial = pl.pallas_call(
            coarse_kernel_product,
            out_shape=jax.ShapeDtypeStruct((per_col, vecs, width), F32),
            in_specs=[vmem, vmem],
            out_specs=vmem,
        )(sums, coarse_kernel)
        if turn_index == 0:
            done = hops[0]
            rotations, partial = take(rotations, got, hops[0], partial)
            for bit in hops[1:]:
                rotations, got, partial = hop(rotations, bit, done, partial)
                rotations, _ = take(rotations, got, bit, got)
                done |= bit
        beside = (rotations, place)
        z, (rotations, spot) = gather_halves(sum_over(partial, "col", BF16).astype(BF16), "row", beside)
        if last:
            turned = rotations.transpose(0, 2, 1)
            hamiltonian = tiles_call(coarse_of, spot, turned, correlations, kernels, cols_total)
            vectors, hamiltonian = lax.optimization_barrier((vectors, hamiltonian))
        shapes = [
            jax.ShapeDtypeStruct((fine_rows, vecs, width), F32),
            jax.ShapeDtypeStruct((vecs, vecs), F32),
        ]
        results = pl.pallas_call(
            functools.partial(step_kernel, rows_total, cols_total, turn_index == 0),
            out_shape=shapes if last else shapes + [sums_shape],
            in_specs=[smem, smem, vmem, vmem, vmem, vmem, vmem],
            out_specs=[vmem] * (2 if last else 3),
            scratch_shapes=[] if last else [total],
        )(coarse_of, place, *z, rotations, energies, vectors)
        vectors = results[0]
        told = results[1] if last else spread(results[1], "row")
        if not last:
            sums = results[2]
    first_bit, *other_bits = bits_of(rows_total)
    told = told + swap(told, "row", first_bit)
    for bit in other_bits:
        told = told + swap(told, "row", bit)
    gram, root = next_root(told, root)
    mine = lax.dynamic_slice_in_dim(vectors, col_index * own, own, 0)
    current = jnp.einsum("kva,vw->kaw", mine, root, precision=HIGHEST, preferred_element_type=F32)
    return hamiltonian, current.reshape(own * width, vecs), gram


def solution(mesh):
    return jax.shard_map(
        per_device,
        mesh=mesh,
        in_specs=(
            P("col", "row", None, None),
            P("col", None, None),
            P(),
            P("row"),
            P(("row", "col"), None),
        ),
        out_specs=(P("row", "col"), P(("row", "col"), None), P()),
        check_vma=False,
    )
```
